512 devices in a mesh: site: 32 (over x_hi, z), expert: 16 (over y, x_lo, core).
Axes of the slice: x: 4 (x_hi: 2, x_lo: 2; x = x_hi * 2 + x_lo), y: 4, z: 16, core: 2. Of those that a mesh axis runs over, the one named last changes fastest.
Arguments:
- out_grads: bfloat16 [2, 32, 2048, 1024], P(None, 'site', 'expert'), may hold values from -6 to 6
- routes: int32 [2, 32, 2048, 1], P(None, 'site', 'expert'), may hold values from 0 to 15; in each aligned block of 128 rows (0 to 127, 128 to 255, ..., all dimensions but the last counted through in order) at most 16 rows name the same one
- hiddens: bfloat16 [2, 32, 16, 256, 512], P(None, 'site', 'expert'), may hold values from -6 to 6
- weights: bfloat16 [32, 16, 512, 1024], P('site', 'expert'), may hold values from -6 to 6
- tracker_offset: bfloat16 [32, 16, 512, 1024], P('site', 'expert'), may hold values from -20 to 20
- partner_bits: int32 [32, 2], P('site'), may hold values from 0 to 1, as said below
Outputs:
- new_weights: bfloat16 [32, 16, 512, 1024], P('site', 'expert')
The draws below stay inside these ranges and needn't reach their ends.
Inputs may be any that keep to these rules, and one draw needn't show every extreme that they name: `routes`: among the 128 tokens of one device in a step no expert is named more than 16 times, a bound that some block reaches. `partner_bits`: site 0 and site 32 - 1 each take the partner ahead in exactly one of the two rounds.
All inputs are finite; a program needn't handle non-finite values.
Results may differ from the reference program's by a relative error of at most 0.0095.
Values may be sent and summed in bfloat16 or wider, within the bound.
A program may use at most 64 MiB of HBM per device.

```python
import math
import jax
import jax.numpy as jnp
import numpy as np
from jax import lax

D = 1024
FF_E = 512
EXP_ROWS = 256
NS_ITERS = 2
STEPS = 2
SITES = 32
EXPERTS = 16
SLOTS = 16
TOK_DEV = 128
TOKENS = 2048


def draw_tracker_offset(key, part):
    key_rows = jax.random.fold_in(key, 11)
    key_cols = jax.random.fold_in(key, 23)
    key_body = jax.random.fold_in(key, 37)
    shape = (SITES, EXPERTS, FF_E, D)
    row_scale = jnp.exp(jax.random.uniform(key_rows, (SITES, EXPERTS, FF_E, 1), jnp.float32) * math.log(10.0))
    col_scale = jnp.exp(jax.random.uniform(key_cols, (SITES, EXPERTS, 1, D), jnp.float32) * math.log(10.0))
    entries = jnp.clip(jax.random.normal(key_body, shape, jnp.float32), -4.0, 4.0) * 0.05
    return (entries * row_scale * col_scale).astype(jnp.bfloat16)


def draw_partner_bits(key, part):
    key_bits = jax.random.fold_in(key, 53)
    bits = jax.random.randint(key_bits, (SITES, 2), 0, 2, jnp.int32)
    rows = jnp.arange(SITES, dtype=jnp.int32)
    at_end = (rows == 0) | (rows == SITES - 1)
    second = jnp.where(at_end, 1 - bits[:, 0], bits[:, 1])
    return jnp.stack([bits[:, 0], second], axis=1)


def levels(own_key, dims, cuts, least, high):
    level = 1.0
    for dim, parts in cuts:
        draws = jax.random.uniform(jax.random.fold_in(jax.random.fold_in(own_key, 6), dim), (parts,), jnp.float32, least / len(cuts), high / len(cuts))
        level = level * jnp.repeat(jnp.exp(draws), dims[dim] // parts).reshape((-1,) + (1,) * (len(dims) - 1 - dim))
    return level


def shared_out(key, own, number, rows, number_of, top, bound, slope):
    order = jax.random.permutation(key, number_of)
    crowded, common = portions_of(number_of, rows * top, bound, slope, True), portions_of(number_of, rows * top, bound, slope, False)
    places = jnp.arange(number_of)

    def named(tallies, turn):
        used = int((tallies > 0).sum())
        fixed = max(1, used // 4)
        passed = fixed + (places - fixed + turn * (used - fixed)) % max(1, number_of - fixed)
        return jnp.zeros((number_of,), jnp.int32).at[order[jnp.where(places < fixed, places, passed)]].set(jnp.asarray(tallies, jnp.int32))

    tallies = jnp.where(number % 4 == 0, named(crowded, number // 4), named(common, number - number // 4 - 1))
    mixed = jax.random.permutation(jax.random.fold_in(own, 3), number_of)
    donor, receiver = mixed[0:number_of // 2 * 2:2], mixed[1:number_of // 2 * 2:2]
    margin = jnp.minimum(tallies[donor] - 1, bound - tallies[receiver]) // 2
    margin = jnp.where((donor == order[0]) | (receiver == order[0]) | (tallies[receiver] == 0), 0, jnp.maximum(margin, 0))
    passed = jax.random.randint(jax.random.fold_in(own, 4), (number_of // 2,), 0, 1 << 20) % (margin + 1)
    tallies = tallies.at[donor].add(-passed).at[receiver].add(passed)
    labels = jnp.searchsorted(jnp.cumsum(tallies), jnp.arange(rows * top), side="right").astype(jnp.int32)
    table = labels.reshape(top, rows).T
    table = table[jax.random.permutation(jax.random.fold_in(own, 1), rows)]
    turn = jax.random.randint(jax.random.fold_in(own, 2), (rows, 1), 0, top)
    return jnp.take_along_axis(table, (jnp.arange(top)[None, :] + turn) % top, axis=1)


def portions_of(amount, total, reach, slope, full):
    weights = [(1 << 20) // math.isqrt(grade ** slope) + 1 for grade in range(1, amount + 1)]
    largest = reach if full else min(reach, max(-(-total // amount), total * weights[0] // sum(weights)))
    least = 1 if total - largest >= amount - 1 else 0
    given, spare = [largest] + [least] * (amount - 1), total - largest - least * (amount - 1)
    while spare > 0:
        movable = [i for i in range(1, amount) if given[i] < largest] or [i for i in range(1, amount) if given[i] < reach]
        whole, remaining = sum([weights[i] for i in movable]), spare
        for i in movable:
            more = min(reach - given[i], max(1, remaining * weights[i] // whole), spare)
            given[i] = given[i] + more
            spare = spare - more
    return np.array(given)


def noise(own_key, shape, scale, most, split=(), kind=jnp.bfloat16):
    level = levels(own_key, shape, split, -0.22, 0.18) if split else 1.0
    values = jax.random.normal(own_key, shape, jnp.float32) * scale * level
    return jnp.minimum(jnp.maximum(values, -most), most).astype(kind)


def setup_inputs(seed: int = 0) -> dict:
    arg_keys = jax.random.split(jax.random.key(seed), 7)
    out_grads = noise(arg_keys[0], (STEPS, SITES, TOKENS, D), 1.0, 6.0, ((1, 32), (2, 16)))
    routes_keys = jax.random.split(jax.random.fold_in(arg_keys[1], 1), STEPS * SITES * TOKENS // TOK_DEV)
    routes_turns = jax.random.permutation(jax.random.fold_in(arg_keys[1], 3), STEPS * SITES * TOKENS // TOK_DEV)
    routes = jax.vmap(lambda own, number: shared_out(jax.random.fold_in(arg_keys[1], 2), own, number, TOK_DEV, EXPERTS, 1, SLOTS, 1))(routes_keys, routes_turns).reshape((STEPS, SITES, TOKENS, 1))
    hiddens = noise(arg_keys[2], (STEPS, SITES, EXPERTS, EXP_ROWS, FF_E), 1.0, 6.0, ((1, 32), (2, 16)))
    weights = noise(arg_keys[3], (SITES, EXPERTS, FF_E, D), 1.0, 6.0, ((0, 32), (1, 16)))
    tracker_offset = draw_tracker_offset(jax.random.fold_in(arg_keys[6], 71), 0)
    partner_bits = draw_partner_bits(jax.random.fold_in(arg_keys[6], 71), 0)
    return {"out_grads": out_grads, "routes": routes, "hiddens": hiddens, "weights": weights, "tracker_offset": tracker_offset, "partner_bits": partner_bits}


coef_a = 3.4445
coef_b = -4.775
coef_c = 2.0315
step_scale = 32.0
weight_hop = 4

def orthogonalize(tracked):
    frobenius = jnp.sqrt(jnp.sum(tracked * tracked))
    current = (tracked / (frobenius + 1e-07)).astype(jnp.bfloat16)
    for repeat in range(NS_ITERS):
        gram_matrix = lax.dot_general(current, current, (((1,), (1,)), ((), ())), preferred_element_type=jnp.float32).astype(jnp.bfloat16)
        squared = jnp.dot(gram_matrix, gram_matrix, preferred_element_type=jnp.float32)
        polynomial = (coef_b * gram_matrix.astype(jnp.float32) + coef_c * squared).astype(jnp.bfloat16)
        current = (coef_a * current.astype(jnp.float32) + jnp.dot(polynomial, current, preferred_element_type=jnp.float32)).astype(jnp.bfloat16)
    return current

def place_rows(gradient, routing):
    owned = (routing[:, None] == jnp.arange(EXPERTS, dtype=jnp.int32)[None, :]).astype(jnp.int32)
    earlier = jnp.cumsum(owned, axis=0) - owned
    position = lax.optimization_barrier(jnp.sum(earlier * owned, axis=1))
    target = routing * SLOTS + position
    selector = (target[None, :] == jnp.arange(EXPERTS * SLOTS, dtype=jnp.int32)[:, None]).astype(jnp.bfloat16)
    return jnp.dot(selector, gradient, preferred_element_type=jnp.float32).astype(jnp.bfloat16)

def site_gradients(inputs):
    gradient, routing, stashed = inputs
    placed = jax.vmap(place_rows)(gradient, routing)
    placed = placed.reshape(EXPERTS, EXPERTS, SLOTS, D)
    arrived = jnp.transpose(placed, (1, 0, 2, 3)).reshape(EXPERTS, EXP_ROWS, D)
    product = jnp.einsum('erf,erd->efd', stashed.astype(jnp.float32), arrived.astype(jnp.float32))
    return (product * (1.0 / math.sqrt(EXP_ROWS))).astype(jnp.bfloat16)

def partner_of(values, distance, direction):
    ahead_value = jnp.roll(values, -distance, axis=0)
    behind = jnp.roll(values, distance, axis=0)
    return jnp.where((direction == 1)[:, None, None, None], ahead_value, behind)

def reference(out_grads, routes, hiddens, weights, tracker_offset, partner_bits):
    offset = tracker_offset
    updates = jnp.zeros((SITES, EXPERTS, FF_E, D), jnp.float32)
    for round_index in range(STEPS):
        gradient = lax.map(site_gradients, (out_grads[round_index].reshape(SITES, EXPERTS, TOK_DEV, D), routes[round_index, :, :, 0].reshape(SITES, EXPERTS, TOK_DEV), hiddens[round_index]))
        distance = 2 ** round_index
        summed = offset.astype(jnp.float32) + gradient.astype(jnp.float32)
        tracked = 0.5 * (summed + partner_of(summed, distance, partner_bits[:, round_index]))
        offset = (tracked - gradient.astype(jnp.float32)).astype(jnp.bfloat16)
        ortho = lax.map(orthogonalize, tracked.reshape(SITES * EXPERTS, FF_E, D))
        updates = updates + ortho.reshape(SITES, EXPERTS, FF_E, D).astype(jnp.float32)
    moved = weights.astype(jnp.float32) - step_scale * updates
    beside_all = jnp.roll(moved, -weight_hop, axis=0) + jnp.roll(moved, weight_hop, axis=0)
    return (0.5 * moved + 0.25 * beside_all).astype(jnp.bfloat16)
```

```python
import math

import jax
import jax.numpy as jnp
from jax import lax
from jax.sharding import PartitionSpec as P

NS_ITERS = 2


coef_a = 3.4445
coef_b = -4.775
coef_c = 2.0315
step_scale = 32.0
weight_hop = 4


def from_behind(block, axis, distance):
    devices = range(lax.axis_size(axis))
    route = [((i - distance) % len(devices), i) for i in devices]
    return lax.ppermute(block, axis, route)


def orthogonalize(tracked):
    frobenius = jnp.sqrt(jnp.sum(tracked * tracked))
    current = (tracked / (frobenius + 1e-07)).astype(jnp.bfloat16)
    for repeat in range(NS_ITERS):
        gram_matrix = lax.dot_general(
            current, current, (((1,), (1,)), ((), ())), preferred_element_type=jnp.float32
        ).astype(jnp.bfloat16)
        squared = jnp.dot(gram_matrix, gram_matrix, preferred_element_type=jnp.float32)
        polynomial = (coef_b * gram_matrix.astype(jnp.float32) + coef_c * squared).astype(
            jnp.bfloat16
        )
        current = (
            coef_a * current.astype(jnp.float32)
            + jnp.dot(polynomial, current, preferred_element_type=jnp.float32)
        ).astype(jnp.bfloat16)
    return current


def place_rows(gradient, routing, experts, slot_count):
    owned = (routing[:, None] == jnp.arange(experts, dtype=jnp.int32)[None, :]).astype(jnp.int32)
    earlier = jnp.cumsum(owned, axis=0) - owned
    position = jnp.sum(earlier * owned, axis=1)
    target = routing * slot_count + position
    selector = (
        target[None, :] == jnp.arange(experts * slot_count, dtype=jnp.int32)[:, None]
    ).astype(jnp.bfloat16)
    placed = jnp.dot(selector, gradient, preferred_element_type=jnp.float32).astype(jnp.bfloat16)
    return placed.reshape(experts, slot_count, gradient.shape[1])


def local_gradient(stashed, arrived):
    product = lax.dot_general(
        stashed, arrived, (((0,), (0,)), ((), ())), preferred_element_type=jnp.float32
    )
    return (product * (1.0 / math.sqrt(stashed.shape[0]))).astype(jnp.bfloat16)


def choose(ahead_value, behind, flag):
    return jnp.where(flag == 1, ahead_value, behind)


def local(out_grads, routes, hiddens, weights, tracker_offset, partner_bits):
    experts = lax.axis_size("expert")
    stashed = hiddens[:, 0, 0]
    step_count = stashed.shape[0]
    slot_rows = stashed.shape[1]
    slot_count = slot_rows // experts
    features = out_grads.shape[-1]
    direction = partner_bits[0]
    weight = weights[0, 0]
    offset = tracker_offset[0, 0]
    placed = [
        place_rows(out_grads[section_index, 0], routes[section_index, 0, :, 0], experts, slot_count)
        for section_index in range(step_count)
    ]
    arrived = [
        lax.all_to_all(outgoing, "expert", split_axis=0, concat_axis=0, tiled=True)
        for outgoing in placed
    ]
    gradients = [
        local_gradient(stashed[section_index], arrived[section_index].reshape(slot_rows, features))
        for section_index in range(step_count)
    ]
    own_updates = jnp.zeros(weight.shape, jnp.float32)
    for section_index in range(step_count):
        distance = 2**section_index
        gradient = gradients[section_index]
        summed = offset.astype(jnp.float32) + gradient.astype(jnp.float32)
        sent = summed.astype(jnp.bfloat16)
        partner_sum = choose(
            from_behind(sent, "site", -distance),
            from_behind(sent, "site", distance),
            direction[section_index],
        ).astype(jnp.float32)
        tracked = 0.5 * (summed + partner_sum)
        offset = (tracked - gradient.astype(jnp.float32)).astype(jnp.bfloat16)
        ortho = orthogonalize(tracked)
        own_updates = own_updates + ortho.astype(jnp.float32)
    updated = weight.astype(jnp.float32) - step_scale * own_updates
    beside_all = from_behind(updated.astype(jnp.bfloat16), "site", -weight_hop).astype(
        updated.dtype
    ) + from_behind(updated.astype(jnp.bfloat16), "site", weight_hop).astype(updated.dtype)
    result = (0.5 * updated + 0.25 * beside_all).astype(jnp.bfloat16)
    return result[None, None]


def solution(mesh):
    in_specs = (
        P(None, "site", "expert", None),
        P(None, "site", "expert", None),
        P(None, "site", "expert", None, None),
        P("site", "expert", None, None),
        P("site", "expert", None, None),
        P("site", None),
    )
    out_specs = P("site", "expert", None, None)
    return jax.shard_map(local, mesh=mesh, in_specs=in_specs, out_specs=out_specs, check_vma=False)
```

```python
import functools
import math

import jax
import jax.numpy as jnp
from jax import lax
from jax.experimental import pallas as pl
from jax.experimental.pallas import tpu as pltpu
from jax.sharding import PartitionSpec as P

MESH = pl.DeviceIdType.MESH
F32 = jnp.float32
BF16 = jnp.bfloat16

coef_a = 3.4445
coef_b = -4.775
coef_c = 2.0315
step_scale = 32.0
HOPS = (1, 2, 4)
CHUNK = 256


def dot_nn(a, b):
    return lax.dot_general(a, b, (((1,), (0,)), ((), ())), preferred_element_type=F32)


def dot_nt(a, b):
    return lax.dot_general(a, b, (((1,), (1,)), ((), ())), preferred_element_type=F32)


def dot_tn(a, b):
    return lax.dot_general(a, b, (((0,), (0,)), ((), ())), preferred_element_type=F32)


def kernel(
    n_sites, n_experts, chunk,
    og_hbm, routes_ref, hid_hbm, w_hbm, off_hbm, bits_ref, out_hbm,
    og, hid, wt, off, placed, arrived, grad, sent, near, tnorm, xmid, moved, out_v,
    gram, gram_b, poly, fro,
    load_sem, a2a_send, a2a_recv, hop_send, hop_recv, out_sem,
):
    site = lax.axis_index("site")
    me = lax.axis_index("expert")
    ff, features = w_hbm.shape
    chunks = features // chunk
    rows = hid.shape[1]
    slots = rows // n_experts
    tokens = og.shape[1]

    def cols(c):
        return pl.ds(pl.multiple_of(c * chunk, chunk), chunk)

    def site_at(distance):
        return lax.rem(site + (distance + n_sites), n_sites)

    def expert_at(d):
        return lax.rem(me + d, n_experts)

    loads = [pltpu.make_async_copy(og_hbm.at[k], og.at[k], load_sem.at[k]) for k in range(2)]
    loads += [pltpu.make_async_copy(hid_hbm.at[k], hid.at[k], load_sem.at[2 + k]) for k in range(2)]

    def off_load(c):
        return pltpu.make_async_copy(off_hbm.at[:, cols(c)], off.at[c], load_sem.at[4 + c])

    def w_load(c):
        return pltpu.make_async_copy(w_hbm.at[:, cols(c)], wt.at[c], load_sem.at[4 + chunks + c])

    loads[0].start()
    loads[2].start()
    for c in range(chunks):
        off_load(c).start()
    loads[1].start()
    loads[3].start()
    for c in range(chunks):
        w_load(c).start()

    barrier = pltpu.get_barrier_semaphore()
    for distance in (1, -1):
        pl.semaphore_signal(barrier, inc=1, device_id={"site": site_at(distance)}, device_id_type=MESH)

    @pl.loop(1, n_experts)
    def _(d):
        pl.semaphore_signal(barrier, inc=1, device_id={"expert": expert_at(d)}, device_id_type=MESH)

    def place(k):
        routing = routes_ref[pl.ds(k, 1), :]
        experts = lax.broadcasted_iota(jnp.int32, (n_experts, tokens), 0)
        owned = jnp.where(experts == routing, 1.0, 0.0)
        early = lax.broadcasted_iota(jnp.int32, (tokens, tokens), 0)
        late = lax.broadcasted_iota(jnp.int32, (tokens, tokens), 1)
        before = jnp.where(early < late, 1.0, 0.0).astype(BF16)
        earlier = dot_nn(owned.astype(BF16), before)
        position = jnp.sum(earlier * owned, axis=0, keepdims=True)
        target = routing.astype(F32) * float(slots) + position
        place_of = lax.broadcasted_iota(jnp.int32, (rows, tokens), 0).astype(F32)
        selector = jnp.where(place_of == target, 1.0, 0.0).astype(BF16)
        placed[k] = dot_nn(selector, og[k]).astype(BF16)
        own = pl.ds(pl.multiple_of(me * slots, slots), slots)
        arrived[k, own, :] = placed[k, own, :]

    def a2a(k, c, d, peer):
        return pltpu.make_async_remote_copy(
            src_ref=placed.at[k, pl.ds(pl.multiple_of(peer * slots, slots), slots), cols(c)],
            dst_ref=arrived.at[k, pl.ds(pl.multiple_of(me * slots, slots), slots), cols(c)],
            send_sem=a2a_send.at[k, c, d - 1],
            recv_sem=a2a_recv.at[k, c, d - 1],
            device_id={"expert": peer},
            device_id_type=MESH,
        )

    def a2a_start(k, c):
        @pl.loop(1, n_experts)
        def _(d):
            a2a(k, c, d, expert_at(d)).start()

    def a2a_wait(k, c):
        @pl.loop(1, n_experts)
        def _(d):
            a2a(k, c, d, expert_at(d)).wait_recv()

    def hop(q, side, c):
        distance = -HOPS[q] if side == 0 else HOPS[q]
        return pltpu.make_async_remote_copy(
            src_ref=sent.at[q, c],
            dst_ref=near.at[q, side, c],
            send_sem=hop_send.at[q, side, c],
            recv_sem=hop_recv.at[q, side, c],
            device_id={"site": site_at(distance)},
            device_id_type=MESH,
        )

    loads[0].wait()
    place(0)
    pl.semaphore_wait(barrier, n_experts + 1)

    @pl.loop(0, chunks)
    def _(c):
        a2a_start(0, c)

    loads[1].wait()
    place(1)
    loads[2].wait()
    loads[3].wait()
    scale = 1.0 / math.sqrt(rows)

    @pl.loop(0, chunks)
    def _(c):
        off_load(c).wait()
        a2a_wait(0, c)
        g = (dot_tn(hid[0], arrived[0, :, cols(c)]) * scale).astype(BF16)
        grad[0, c] = g
        sent[0, c] = (off[c].astype(F32) + g.astype(F32)).astype(BF16)
        hop(0, 0, c).start()
        hop(0, 1, c).start()
        a2a_start(1, c)

    @pl.loop(0, chunks)
    def _(c):
        a2a_wait(1, c)
        grad[1, c] = (dot_tn(hid[1], arrived[1, :, cols(c)]) * scale).astype(BF16)

    def partner(q, c):
        flag = bits_ref[0, q]
        return jnp.where(flag == 1, near[q, 0, c].astype(F32), near[q, 1, c].astype(F32))

    def hop_wait(q, c):
        hop(q, 0, c).wait_recv()
        hop(q, 1, c).wait_recv()

    fro[...] = jnp.zeros_like(fro)

    @pl.loop(0, chunks)
    def _(c):
        hop_wait(0, c)
        g = grad[0, c].astype(F32)
        summed = off[c].astype(F32) + g
        tracked = 0.5 * (summed + partner(0, c))
        second = (tracked - g).astype(BF16).astype(F32) + grad[1, c].astype(F32)
        sent[1, c] = second.astype(BF16)
        hop(1, 0, c).start()
        hop(1, 1, c).start()
        off[c] = (tracked - g).astype(BF16)
        tnorm[c] = tracked.astype(BF16)
        fro[...] += jnp.sum(tracked * tracked, axis=0, keepdims=True)

    def newton_schulz(finish):
        r = 1.0 / (jnp.sqrt(jnp.sum(fro[...], axis=1, keepdims=True)) + 1e-07)
        gram_b[...] = (gram[...] * (r * r)).astype(BF16)

        def polynomial():
            gb = gram_b[...]
            poly[...] = (coef_b * gb.astype(F32) + coef_c * dot_nn(gb, gb)).astype(BF16)

        polynomial()
        gram[...] = jnp.zeros_like(gram)

        @pl.loop(0, chunks)
        def _(c):
            t = tnorm[c]
            x = (r * (coef_a * t.astype(F32) + dot_nn(poly[...], t))).astype(BF16)
            xmid[c] = x
            gram[...] += dot_nt(x, x)

        gram_b[...] = gram[...].astype(BF16)
        polynomial()

        @pl.loop(0, chunks)
        def _(c):
            x = xmid[c]
            finish(c, (coef_a * x.astype(F32) + dot_nn(poly[...], x)).astype(BF16).astype(F32))

    gram[...] = jnp.zeros_like(gram)

    @pl.loop(0, chunks)
    def _(c):
        t = tnorm[c]
        gram[...] += dot_nt(t, t)

    for c in range(chunks):
        w_load(c).wait()

    def finish_first(c, ortho):
        moved[c] = wt[c].astype(F32) - step_scale * ortho

    newton_schulz(finish_first)

    fro[...] = jnp.zeros_like(fro)
    gram[...] = jnp.zeros_like(gram)

    @pl.loop(0, chunks)
    def _(c):
        hop_wait(1, c)
        summed = off[c].astype(F32) + grad[1, c].astype(F32)
        tracked = 0.5 * (summed + partner(1, c))
        fro[...] += jnp.sum(tracked * tracked, axis=0, keepdims=True)
        t = tracked.astype(BF16)
        tnorm[c] = t
        gram[...] += dot_nt(t, t)

    def finish_second(c, ortho):
        m = moved[c] - step_scale * ortho
        sent[2, c] = m.astype(BF16)
        hop(2, 0, c).start()
        hop(2, 1, c).start()
        moved[c] = m

    newton_schulz(finish_second)

    def out_copy(c):
        return pltpu.make_async_copy(out_v.at[c], out_hbm.at[:, cols(c)], out_sem.at[c])

    @pl.loop(0, chunks)
    def _(c):
        hop_wait(2, c)
        beside = near[2, 0, c].astype(F32) + near[2, 1, c].astype(F32)
        out_v[c] = (0.5 * moved[c] + 0.25 * beside).astype(BF16)
        out_copy(c).start()

    @pl.loop(0, chunks)
    def _(c):
        for k in range(2):
            @pl.loop(1, n_experts)
            def _(d):
                a2a(k, c, d, expert_at(d)).wait_send()
        for q in range(3):
            for side in range(2):
                hop(q, side, c).wait_send()
        out_copy(c).wait()


def local(out_grads, routes, hiddens, weights, tracker_offset, partner_bits, chunk=CHUNK):
    n_experts = lax.axis_size("expert")
    n_sites = lax.axis_size("site")
    steps, _, tokens, features = out_grads.shape
    _, _, _, rows, ff = hiddens.shape
    chunks = features // chunk
    block = (chunks, ff, chunk)
    hbm = pl.BlockSpec(memory_space=pl.ANY)
    result = pl.pallas_call(
        functools.partial(kernel, n_sites, n_experts, chunk),
        out_shape=jax.ShapeDtypeStruct((ff, features), BF16),
        in_specs=[
            hbm,
            pl.BlockSpec(memory_space=pltpu.VMEM),
            hbm,
            hbm,
            hbm,
            pl.BlockSpec(memory_space=pltpu.SMEM),
        ],
        out_specs=hbm,
        scratch_shapes=[
            pltpu.VMEM((2, tokens, features), BF16),
            pltpu.VMEM((2, rows, ff), BF16),
            pltpu.VMEM(block, BF16),
            pltpu.VMEM(block, BF16),
            pltpu.VMEM((2, rows, features), BF16),
            pltpu.VMEM((2, rows, features), BF16),
            pltpu.VMEM((2,) + block, BF16),
            pltpu.VMEM((3,) + block, BF16),
            pltpu.VMEM((3, 2) + block, BF16),
            pltpu.VMEM(block, BF16),
            pltpu.VMEM(block, BF16),
            pltpu.VMEM(block, F32),
            pltpu.VMEM(block, BF16),
            pltpu.VMEM((ff, ff), F32),
            pltpu.VMEM((ff, ff), BF16),
            pltpu.VMEM((ff, ff), BF16),
            pltpu.VMEM((1, chunk), F32),
            pltpu.SemaphoreType.DMA((4 + 2 * chunks,)),
            pltpu.SemaphoreType.DMA((2, chunks, n_experts - 1)),
            pltpu.SemaphoreType.DMA((2, chunks, n_experts - 1)),
            pltpu.SemaphoreType.DMA((3, 2, chunks)),
            pltpu.SemaphoreType.DMA((3, 2, chunks)),
            pltpu.SemaphoreType.DMA((chunks,)),
        ],
        compiler_params=pltpu.CompilerParams(collective_id=0, has_side_effects=True),
        name="gossip_muon",
    )(
        out_grads[:, 0],
        routes[:, 0, :, 0],
        hiddens[:, 0, 0],
        weights[0, 0],
        tracker_offset[0, 0],
        partner_bits,
    )
    return result[None, None]


def solution(mesh):
    in_specs = (
        P(None, "site", "expert", None),
        P(None, "site", "expert", None),
        P(None, "site", "expert", None, None),
        P("site", "expert", None, None),
        P("site", "expert", None, None),
        P("site", None),
    )
    out_specs = P("site", "expert", None, None)
    return jax.shard_map(local, mesh=mesh, in_specs=in_specs, out_specs=out_specs, check_vma=False)
```

```python
import functools
import math

import jax
import jax.numpy as jnp
from jax import lax
from jax.experimental import pallas as pl
from jax.experimental.pallas import tpu as pltpu
from jax.sharding import PartitionSpec as P

MESH = pl.DeviceIdType.MESH
F32 = jnp.float32
BF16 = jnp.bfloat16

coef_a = 3.4445
coef_b = -4.775
coef_c = 2.0315
step_scale = 32.0
HOPS = (1, 2, 4)
BASE = (0, 1, 3)
RELAY = (0, 0, 1)
CHUNK = 256


def dot_nn(a, b):
    return lax.dot_general(a, b, (((1,), (0,)), ((), ())), preferred_element_type=F32)


def dot_nt(a, b):
    return lax.dot_general(a, b, (((1,), (1,)), ((), ())), preferred_element_type=F32)


def dot_tn(a, b):
    return lax.dot_general(a, b, (((0,), (0,)), ((), ())), preferred_element_type=F32)


def kernel(
    n_sites, n_experts, chunk,
    og_hbm, routes_ref, hid_hbm, w_hbm, off_hbm, bits_ref, out_ref,
    og, hid, wt, off, placed, arrived, grad, sent, relay, near, tnorm, xmid, moved,
    gram, gram_b, poly, fro,
    load_sem, a2a_send, a2a_recv, hop_send, hop_recv, turn,
):
    site = lax.axis_index("site")
    me = lax.axis_index("expert")
    ff, features = w_hbm.shape
    chunks = features // chunk
    rows = hid.shape[1]
    slots = rows // n_experts
    tokens = og.shape[1]

    def cols(c):
        return pl.ds(pl.multiple_of(c * chunk, chunk), chunk)

    ring = n_sites // 2
    lane = site // ring
    spot = lax.rem(site, ring)

    far = HOPS[-1]
    core = lax.rem(me, 2)
    chip = me // 2
    n_chips = n_experts // 2

    def ring_at(distance, cross=0):
        return lax.rem(lane + cross, 2) * ring + lax.rem(spot + (distance + ring), ring)

    loads = [pltpu.make_async_copy(og_hbm.at[k], og.at[k], load_sem.at[k]) for k in range(2)]
    loads += [pltpu.make_async_copy(hid_hbm.at[k], hid.at[k], load_sem.at[2 + k]) for k in range(2)]

    def off_load(c):
        return pltpu.make_async_copy(off_hbm.at[:, cols(c)], off.at[c], load_sem.at[4 + c])

    def w_load(c):
        return pltpu.make_async_copy(w_hbm.at[:, cols(c)], wt.at[c], load_sem.at[4 + chunks + c])

    loads[0].start()
    loads[2].start()
    for c in range(chunks):
        off_load(c).start()
    loads[1].start()
    loads[3].start()
    for c in range(chunks):
        w_load(c).start()

    barrier = pltpu.get_barrier_semaphore()
    def greet(device_id):
        pl.semaphore_signal(barrier, inc=1, device_id=device_id, device_id_type=MESH)

    for way in (1, -1):
        greet({"site": ring_at(way)})
    pl.when(spot < far)(lambda: greet({"site": ring_at(-1, 1)}))
    pl.when(spot >= ring - far)(lambda: greet({"site": ring_at(1, 1)}))

    @pl.loop(1, n_experts)
    def _(d):
        greet({"expert": lax.rem(me + d, n_experts)})

    crossings = jnp.where(lax.rem(spot + 1, ring) < far, 1, 0) + jnp.where(lax.rem(ring - spot, ring) < far, 1, 0)

    def place(k):
        routing = routes_ref[pl.ds(k, 1), :]
        experts = lax.broadcasted_iota(jnp.int32, (n_experts, tokens), 0)
        owned = jnp.where(experts == routing, 1.0, 0.0)
        early = lax.broadcasted_iota(jnp.int32, (tokens, tokens), 0)
        late = lax.broadcasted_iota(jnp.int32, (tokens, tokens), 1)
        before = jnp.where(early < late, 1.0, 0.0).astype(BF16)
        earlier = dot_nn(owned.astype(BF16), before)
        position = jnp.sum(earlier * owned, axis=0, keepdims=True)
        target = routing.astype(F32) * float(slots) + position
        place_of = lax.broadcasted_iota(jnp.int32, (rows, tokens), 0).astype(F32)
        selector = jnp.where(place_of == target, 1.0, 0.0).astype(BF16)
        placed[k] = dot_nn(selector, og[k]).astype(BF16)
        own = pl.ds(pl.multiple_of(me * slots, slots), slots)
        arrived[k, own, :] = placed[k, own, :]

    def a2a(k, c, i, to):
        peer = lax.rem(chip + i, n_chips) * 2 + to
        return pltpu.make_async_remote_copy(
            src_ref=placed.at[k, pl.ds(pl.multiple_of(peer * slots, slots), slots), cols(c)],
            dst_ref=arrived.at[k, pl.ds(pl.multiple_of(me * slots, slots), slots), cols(c)],
            send_sem=a2a_send.at[k, c, 2 * i + to],
            recv_sem=a2a_recv.at[k, c, 2 * i + core],
            device_id={"expert": peer},
            device_id_type=MESH,
        )

    def a2a_recv_wait(k, c, i, source):
        place = arrived.at[k, pl.ds(0, slots), cols(c)]
        pltpu.make_async_copy(place, place, a2a_recv.at[k, c, 2 * i + source]).wait()

    def a2a_start(k):
        for to in range(2):

            @pl.loop(0, chunks)
            def _(c):
                pl.when(core != to)(lambda: a2a(k, c, 0, to).start())

                @pl.loop(1, n_chips)
                def _(i):
                    a2a(k, c, i, to).start()

    def a2a_wait(k, c):
        a2a_recv_wait(k, c, 0, 1 - core)

        @pl.loop(1, n_chips)
        def _(i):
            for source in range(2):
                a2a_recv_wait(k, c, i, source)

    def a2a_end(k, c):
        a2a(k, c, 0, 1 - core).wait_send()

        @pl.loop(1, n_chips)
        def _(i):
            for to in range(2):
                a2a(k, c, i, to).wait_send()

    def crosses(q, side):
        beyond = lax.rem(spot + 1, ring) if side == 1 else lax.rem(ring - spot, ring)
        return beyond < HOPS[q]

    def hop(q, step, side, c):
        way = 2 * side - 1
        if step < HOPS[q] - 1:
            dst, target = relay.at[RELAY[q] + step, side, c], ring_at(way)
        else:
            dst, target = near.at[q, side, c], ring_at(way, jnp.where(crosses(q, side), 1, 0))
        return pltpu.make_async_remote_copy(
            src_ref=sent.at[q, c] if step == 0 else relay.at[RELAY[q] + step - 1, side, c],
            dst_ref=dst,
            send_sem=hop_send.at[BASE[q] + step, side, c],
            recv_sem=hop_recv.at[BASE[q] + step, side, c],
            device_id={"site": target},
            device_id_type=MESH,
        )

    def hop_start(q, c):
        for side in range(2):
            hop(q, 0, side, c).start()

    def first_start(c):
        for side in range(2):
            pl.when(spot != (0, ring - 1)[side])(lambda: hop(0, 0, side, c).start())

    def seam_start():
        for side in range(2):

            @pl.when(spot == (0, ring - 1)[side])
            def _():
                @pl.loop(0, chunks)
                def _(c):
                    hop(0, 0, side, c).start()

    def hop_wait(q, c):
        for side in range(2):
            hop(q, HOPS[q] - 1, side, c).wait_recv()

    def pass_on(q):
        for step in range(1, HOPS[q]):
            @pl.loop(0, chunks)
            def _(c):
                for side in range(2):
                    hop(q, step - 1, side, c).wait_recv()
                    hop(q, step, side, c).start()

    loads[0].wait()
    place(0)
    pl.semaphore_wait(barrier, n_experts + 1 + crossings)

    a2a_start(0)
    loads[1].wait()
    place(1)

    a2a_start(1)
    loads[2].wait()
    loads[3].wait()
    scale = 1.0 / math.sqrt(rows)

    @pl.loop(0, chunks)
    def _(c):
        off_load(c).wait()
        a2a_wait(0, c)
        g = (dot_tn(hid[0], arrived[0, :, cols(c)]) * scale).astype(BF16)
        grad[0, c] = g
        sent[0, c] = (off[c].astype(F32) + g.astype(F32)).astype(BF16)
        first_start(c)

    seam_start()

    def partner(q, c):
        flag = bits_ref[0, q]
        return jnp.where(flag == 1, near[q, 0, c].astype(F32), near[q, 1, c].astype(F32))

    fro[...] = jnp.zeros_like(fro)

    @pl.loop(0, chunks)
    def _(c):
        a2a_wait(1, c)
        late = (dot_tn(hid[1], arrived[1, :, cols(c)]) * scale).astype(BF16)
        grad[1, c] = late
        hop_wait(0, c)
        g = grad[0, c].astype(F32)
        summed = off[c].astype(F32) + g
        tracked = 0.5 * (summed + partner(0, c))
        second = (tracked - g).astype(BF16).astype(F32) + late.astype(F32)
        sent[1, c] = second.astype(BF16)
        hop_start(1, c)
        off[c] = (tracked - g).astype(BF16)
        tnorm[c] = tracked.astype(BF16)
        fro[...] += jnp.sum(tracked * tracked, axis=0, keepdims=True)

    def newton_schulz(finish):
        r = 1.0 / (jnp.sqrt(jnp.sum(fro[...], axis=1, keepdims=True)) + 1e-07)
        gram_b[...] = (gram[...] * (r * r)).astype(BF16)

        def polynomial():
            gb = gram_b[...]
            poly[...] = (coef_b * gb.astype(F32) + coef_c * dot_nn(gb, gb)).astype(BF16)

        polynomial()
        gram[...] = jnp.zeros_like(gram)

        @pl.loop(0, chunks)
        def _(c):
            t = tnorm[c]
            x = (r * (coef_a * t.astype(F32) + dot_nn(poly[...], t))).astype(BF16)
            xmid[c] = x
            gram[...] += dot_nt(x, x)

        gram_b[...] = gram[...].astype(BF16)
        polynomial()

        @pl.loop(0, chunks)
        def _(c):
            x = xmid[c]
            finish(c, (coef_a * x.astype(F32) + dot_nn(poly[...], x)).astype(BF16).astype(F32))

    gram[...] = jnp.zeros_like(gram)

    @pl.loop(0, chunks)
    def _(c):
        t = tnorm[c]
        gram[...] += dot_nt(t, t)

    for c in range(chunks):
        w_load(c).wait()

    def finish_first(c, ortho):
        moved[c] = wt[c].astype(F32) - step_scale * ortho

    newton_schulz(finish_first)

    pl.when(core == 1)(lambda: pl.semaphore_wait(turn, 1))
    pass_on(1)

    @pl.when(core == 0)
    def _():
        for side in range(2):
            hop(1, 1, side, chunks - 2).wait_send()
        pl.semaphore_signal(turn, inc=1, device_id={"expert": me + 1}, device_id_type=MESH)

    fro[...] = jnp.zeros_like(fro)
    gram[...] = jnp.zeros_like(gram)

    @pl.loop(0, chunks)
    def _(c):
        hop_wait(1, c)
        summed = off[c].astype(F32) + grad[1, c].astype(F32)
        tracked = 0.5 * (summed + partner(1, c))
        fro[...] += jnp.sum(tracked * tracked, axis=0, keepdims=True)
        t = tracked.astype(BF16)
        tnorm[c] = t
        gram[...] += dot_nt(t, t)

    def finish_second(c, ortho):
        m = moved[c] - step_scale * ortho
        sent[2, c] = m.astype(BF16)
        hop_start(2, c)
        moved[c] = m

    newton_schulz(finish_second)
    pass_on(2)

    @pl.loop(0, chunks)
    def _(c):
        hop_wait(2, c)
        beside = near[2, 0, c].astype(F32) + near[2, 1, c].astype(F32)
        out_ref[:, cols(c)] = (0.5 * moved[c] + 0.25 * beside).astype(BF16)

    @pl.loop(0, chunks)
    def _(c):
        for k in range(2):
            a2a_end(k, c)
        for q in range(3):
            for step in range(HOPS[q]):
                for side in range(2):
                    if (q, step) == (1, 1):
                        waited = (core == 0) & (c == chunks - 2)
                        pl.when(jnp.logical_not(waited))(lambda: hop(1, 1, side, c).wait_send())
                    else:
                        hop(q, step, side, c).wait_send()


def local(out_grads, routes, hiddens, weights, tracker_offset, partner_bits, chunk=CHUNK):
    n_experts = lax.axis_size("expert")
    n_sites = lax.axis_size("site")
    steps, _, tokens, features = out_grads.shape
    _, _, _, rows, ff = hiddens.shape
    chunks = features // chunk
    block = (chunks, ff, chunk)
    hbm = pl.BlockSpec(memory_space=pl.ANY)
    result = pl.pallas_call(
        functools.partial(kernel, n_sites, n_experts, chunk),
        out_shape=pltpu.VMEM((ff, features), BF16),
        in_specs=[
            hbm,
            pl.BlockSpec(memory_space=pltpu.VMEM),
            hbm,
            hbm,
            hbm,
            pl.BlockSpec(memory_space=pltpu.SMEM),
        ],
        out_specs=pl.BlockSpec(memory_space=pltpu.VMEM),
        scratch_shapes=[
            pltpu.VMEM((2, tokens, features), BF16),
            pltpu.VMEM((2, rows, ff), BF16),
            pltpu.VMEM(block, BF16),
            pltpu.VMEM(block, BF16),
            pltpu.VMEM((2, rows, features), BF16),
            pltpu.VMEM((2, rows, features), BF16),
            pltpu.VMEM((2,) + block, BF16),
            pltpu.VMEM((3,) + block, BF16),
            pltpu.VMEM((4, 2) + block, BF16),
            pltpu.VMEM((3, 2) + block, BF16),
            pltpu.VMEM(block, BF16),
            pltpu.VMEM(block, BF16),
            pltpu.VMEM(block, F32),
            pltpu.VMEM((ff, ff), F32),
            pltpu.VMEM((ff, ff), BF16),
            pltpu.VMEM((ff, ff), BF16),
            pltpu.VMEM((1, chunk), F32),
            pltpu.SemaphoreType.DMA((4 + 2 * chunks,)),
            pltpu.SemaphoreType.DMA((2, chunks, n_experts)),
            pltpu.SemaphoreType.DMA((2, chunks, n_experts)),
            pltpu.SemaphoreType.DMA((7, 2, chunks)),
            pltpu.SemaphoreType.DMA((7, 2, chunks)),
            pltpu.SemaphoreType.REGULAR,
        ],
        compiler_params=pltpu.CompilerParams(collective_id=0, has_side_effects=True, vmem_limit_bytes=61 << 20),
        name="gossip_muon",
    )(
        out_grads[:, 0],
        routes[:, 0, :, 0],
        hiddens[:, 0, 0],
        weights[0, 0],
        tracker_offset[0, 0],
        partner_bits,
    )
    return result[None, None]


def solution(mesh):
    in_specs = (
        P(None, "site", "expert", None),
        P(None, "site", "expert", None),
        P(None, "site", "expert", None, None),
        P("site", "expert", None, None),
        P("site", "expert", None, None),
        P("site", None),
    )
    out_specs = P("site", "expert", None, None)
    return jax.shard_map(local, mesh=mesh, in_specs=in_specs, out_specs=out_specs, check_vma=False)
```

```python
import functools
import math

import jax
import jax.numpy as jnp
from jax import lax
from jax.experimental import pallas as pl
from jax.experimental.pallas import tpu as pltpu
from jax.sharding import PartitionSpec as P

MESH = pl.DeviceIdType.MESH
F32 = jnp.float32
BF16 = jnp.bfloat16

coef_a = 3.4445
coef_b = -4.775
coef_c = 2.0315
step_scale = 32.0
HOPS = (1, 2, 4)
BASE = (0, 1, 3)
RELAY = (0, 0, 1)
CHUNK = 256


def dot_nn(a, b):
    return lax.dot_general(a, b, (((1,), (0,)), ((), ())), preferred_element_type=F32)


def dot_nt(a, b):
    return lax.dot_general(a, b, (((1,), (1,)), ((), ())), preferred_element_type=F32)


def kernel(
    n_sites, n_experts, chunk,
    og_hbm, routes_ref, hid_hbm, w_hbm, off_hbm, bits_ref, out_ref,
    og, hid, hid_t, wt, off, placed, arrived, grad, sent, relay, near, tnorm, xmid, moved,
    gram, gram_b, poly, fro,
    load_sem, a2a_send, a2a_recv, hop_send, hop_recv, turn,
):
    site = lax.axis_index("site")
    me = lax.axis_index("expert")
    ff, features = w_hbm.shape
    chunks = features // chunk
    rows = hid.shape[1]
    slots = rows // n_experts
    tokens = og.shape[1]

    def cols(c):
        return pl.ds(pl.multiple_of(c * chunk, chunk), chunk)

    ring = n_sites // 2
    lane = site // ring
    spot = lax.rem(site, ring)

    far = HOPS[-1]
    core = lax.rem(me, 2)
    chip = me // 2
    n_chips = n_experts // 2

    def ring_at(distance, cross=0):
        return lax.rem(lane + cross, 2) * ring + lax.rem(spot + (distance + ring), ring)

    loads = [pltpu.make_async_copy(og_hbm.at[k], og.at[k], load_sem.at[k]) for k in range(2)]
    loads += [pltpu.make_async_copy(hid_hbm.at[k], hid.at[k], load_sem.at[2 + k]) for k in range(2)]

    def off_load(c):
        return pltpu.make_async_copy(off_hbm.at[:, cols(c)], off.at[c], load_sem.at[4 + c])

    def w_load(c):
        return pltpu.make_async_copy(w_hbm.at[:, cols(c)], wt.at[c], load_sem.at[4 + chunks + c])

    loads[0].start()
    loads[2].start()
    for c in range(chunks):
        off_load(c).start()
    loads[1].start()
    loads[3].start()
    for c in range(chunks):
        w_load(c).start()

    barrier = pltpu.get_barrier_semaphore()
    def greet(device_id):
        pl.semaphore_signal(barrier, inc=1, device_id=device_id, device_id_type=MESH)

    for way in (1, -1):
        greet({"site": ring_at(way)})
    pl.when(spot < far)(lambda: greet({"site": ring_at(-1, 1)}))
    pl.when(spot >= ring - far)(lambda: greet({"site": ring_at(1, 1)}))

    @pl.loop(1, n_experts)
    def _(d):
        greet({"expert": lax.rem(me + d, n_experts)})

    crossings = jnp.where(lax.rem(spot + 1, ring) < far, 1, 0) + jnp.where(lax.rem(ring - spot, ring) < far, 1, 0)

    def place(k):
        routing = routes_ref[pl.ds(k, 1), :]
        experts = lax.broadcasted_iota(jnp.int32, (n_experts, tokens), 0)
        owned = jnp.where(experts == routing, 1.0, 0.0)
        early = lax.broadcasted_iota(jnp.int32, (tokens, tokens), 0)
        late = lax.broadcasted_iota(jnp.int32, (tokens, tokens), 1)
        before = jnp.where(early < late, 1.0, 0.0).astype(BF16)
        earlier = dot_nn(owned.astype(BF16), before)
        position = jnp.sum(earlier * owned, axis=0, keepdims=True)
        target = routing.astype(F32) * float(slots) + position
        place_of = lax.broadcasted_iota(jnp.int32, (rows, tokens), 0).astype(F32)
        selector = jnp.where(place_of == target, 1.0, 0.0).astype(BF16)
        placed[k] = dot_nn(selector, og[k]).astype(BF16)
        own = pl.ds(pl.multiple_of(me * slots, slots), slots)
        arrived[k, own, :] = placed[k, own, :]

    def a2a(k, c, i, to):
        peer = lax.rem(chip + i, n_chips) * 2 + to
        return pltpu.make_async_remote_copy(
            src_ref=placed.at[k, pl.ds(pl.multiple_of(peer * slots, slots), slots), cols(c)],
            dst_ref=arrived.at[k, pl.ds(pl.multiple_of(me * slots, slots), slots), cols(c)],
            send_sem=a2a_send.at[k, c, 2 * i + to],
            recv_sem=a2a_recv.at[k, c, 2 * i + core],
            device_id={"expert": peer},
            device_id_type=MESH,
        )

    def a2a_recv_wait(k, c, i, source):
        place = arrived.at[k, pl.ds(0, slots), cols(c)]
        pltpu.make_async_copy(place, place, a2a_recv.at[k, c, 2 * i + source]).wait()

    def a2a_start(k):
        for to in range(2):

            @pl.loop(0, chunks)
            def _(c):
                pl.when(core != to)(lambda: a2a(k, c, 0, to).start())

                @pl.loop(1, n_chips)
                def _(i):
                    a2a(k, c, i, to).start()

    def a2a_wait(k, c):
        a2a_recv_wait(k, c, 0, 1 - core)

        @pl.loop(1, n_chips)
        def _(i):
            for source in range(2):
                a2a_recv_wait(k, c, i, source)

    def a2a_end(k, c):
        a2a(k, c, 0, 1 - core).wait_send()

        @pl.loop(1, n_chips)
        def _(i):
            for to in range(2):
                a2a(k, c, i, to).wait_send()

    def crosses(q, side):
        beyond = lax.rem(spot + 1, ring) if side == 1 else lax.rem(ring - spot, ring)
        return beyond < HOPS[q]

    def hop(q, step, side, c):
        way = 2 * side - 1
        if step < HOPS[q] - 1:
            dst, target = relay.at[RELAY[q] + step, side, c], ring_at(way)
        else:
            dst, target = near.at[q, side, c], ring_at(way, jnp.where(crosses(q, side), 1, 0))
        return pltpu.make_async_remote_copy(
            src_ref=sent.at[q, c] if step == 0 else relay.at[RELAY[q] + step - 1, side, c],
            dst_ref=dst,
            send_sem=hop_send.at[BASE[q] + step, side, c],
            recv_sem=hop_recv.at[BASE[q] + step, side, c],
            device_id={"site": target},
            device_id_type=MESH,
        )

    def hop_start(q, c):
        for side in range(2):
            hop(q, 0, side, c).start()

    def first_start(c):
        for side in range(2):
            pl.when(spot != (0, ring - 1)[side])(lambda: hop(0, 0, side, c).start())

    def seam_start():
        for side in range(2):

            @pl.when(spot == (0, ring - 1)[side])
            def _():
                @pl.loop(0, chunks)
                def _(c):
                    hop(0, 0, side, c).start()

    def hop_wait(q, c):
        for side in range(2):
            hop(q, HOPS[q] - 1, side, c).wait_recv()

    def pass_on(q):
        for step in range(1, HOPS[q]):
            @pl.loop(0, chunks)
            def _(c):
                for side in range(2):
                    hop(q, step - 1, side, c).wait_recv()
                    hop(q, step, side, c).start()

    loads[0].wait()
    place(0)
    pl.semaphore_wait(barrier, n_experts + 1 + crossings)

    a2a_start(0)
    loads[2].wait()
    hid_t[0] = hid[0].T
    loads[1].wait()
    place(1)

    a2a_start(1)
    scale = 1.0 / math.sqrt(rows)

    @pl.loop(0, chunks)
    def _(c):
        off_load(c).wait()
        a2a_wait(0, c)
        g = (dot_nn(hid_t[0], arrived[0, :, cols(c)]) * scale).astype(BF16)
        grad[0, c] = g
        sent[0, c] = (off[c].astype(F32) + g.astype(F32)).astype(BF16)
        first_start(c)

    seam_start()
    loads[3].wait()
    hid_t[1] = hid[1].T

    def partner(q, c):
        flag = bits_ref[0, q]
        return jnp.where(flag == 1, near[q, 0, c].astype(F32), near[q, 1, c].astype(F32))

    fro[...] = jnp.zeros_like(fro)

    @pl.loop(0, chunks)
    def _(c):
        a2a_wait(1, c)
        late = (dot_nn(hid_t[1], arrived[1, :, cols(c)]) * scale).astype(BF16)
        grad[1, c] = late
        hop_wait(0, c)
        g = grad[0, c].astype(F32)
        summed = off[c].astype(F32) + g
        tracked = 0.5 * (summed + partner(0, c))
        second = (tracked - g).astype(BF16).astype(F32) + late.astype(F32)
        sent[1, c] = second.astype(BF16)
        hop_start(1, c)
        off[c] = (tracked - g).astype(BF16)
        tnorm[c] = tracked.astype(BF16)
        fro[...] += jnp.sum(tracked * tracked, axis=0, keepdims=True)

    def newton_schulz(finish):
        r = 1.0 / (jnp.sqrt(jnp.sum(fro[...], axis=1, keepdims=True)) + 1e-07)
        gram_b[...] = (gram[...] * (r * r)).astype(BF16)

        def polynomial():
            gb = gram_b[...]
            poly[...] = (coef_b * gb.astype(F32) + coef_c * dot_nn(gb, gb)).astype(BF16)

        polynomial()
        gram[...] = jnp.zeros_like(gram)

        @pl.loop(0, chunks)
        def _(c):
            t = tnorm[c]
            x = (r * (coef_a * t.astype(F32) + dot_nn(poly[...], t))).astype(BF16)
            xmid[c] = x
            gram[...] += dot_nt(x, x)

        gram_b[...] = gram[...].astype(BF16)
        polynomial()

        @pl.loop(0, chunks)
        def _(c):
            x = xmid[c]
            finish(c, (coef_a * x.astype(F32) + dot_nn(poly[...], x)).astype(BF16).astype(F32))

    gram[...] = jnp.zeros_like(gram)

    @pl.loop(0, chunks)
    def _(c):
        t = tnorm[c]
        gram[...] += dot_nt(t, t)

    for c in range(chunks):
        w_load(c).wait()

    def finish_first(c, ortho):
        moved[c] = wt[c].astype(F32) - step_scale * ortho

    newton_schulz(finish_first)

    pl.when(core == 1)(lambda: pl.semaphore_wait(turn, 1))
    pass_on(1)

    @pl.when(core == 0)
    def _():
        for side in range(2):
            hop(1, 1, side, chunks - 2).wait_send()
        pl.semaphore_signal(turn, inc=1, device_id={"expert": me + 1}, device_id_type=MESH)

    fro[...] = jnp.zeros_like(fro)
    gram[...] = jnp.zeros_like(gram)

    @pl.loop(0, chunks)
    def _(c):
        hop_wait(1, c)
        summed = off[c].astype(F32) + grad[1, c].astype(F32)
        tracked = 0.5 * (summed + partner(1, c))
        fro[...] += jnp.sum(tracked * tracked, axis=0, keepdims=True)
        t = tracked.astype(BF16)
        tnorm[c] = t
        gram[...] += dot_nt(t, t)

    def finish_second(c, ortho):
        m = moved[c] - step_scale * ortho
        sent[2, c] = m.astype(BF16)
        hop_start(2, c)
        moved[c] = m

    newton_schulz(finish_second)
    pass_on(2)

    @pl.loop(0, chunks)
    def _(c):
        hop_wait(2, c)
        beside = near[2, 0, c].astype(F32) + near[2, 1, c].astype(F32)
        out_ref[:, cols(c)] = (0.5 * moved[c] + 0.25 * beside).astype(BF16)

    @pl.loop(0, chunks)
    def _(c):
        for k in range(2):
            a2a_end(k, c)
        for q in range(3):
            for step in range(HOPS[q]):
                for side in range(2):
                    if (q, step) == (1, 1):
                        waited = (core == 0) & (c == chunks - 2)
                        pl.when(jnp.logical_not(waited))(lambda: hop(1, 1, side, c).wait_send())
                    else:
                        hop(q, step, side, c).wait_send()


def local(out_grads, routes, hiddens, weights, tracker_offset, partner_bits, chunk=CHUNK):
    n_experts = lax.axis_size("expert")
    n_sites = lax.axis_size("site")
    steps, _, tokens, features = out_grads.shape
    _, _, _, rows, ff = hiddens.shape
    chunks = features // chunk
    block = (chunks, ff, chunk)
    hbm = pl.BlockSpec(memory_space=pl.ANY)
    result = pl.pallas_call(
        functools.partial(kernel, n_sites, n_experts, chunk),
        out_shape=pltpu.VMEM((ff, features), BF16),
        in_specs=[
            hbm,
            pl.BlockSpec(memory_space=pltpu.VMEM),
            hbm,
            hbm,
            hbm,
            pl.BlockSpec(memory_space=pltpu.SMEM),
        ],
        out_specs=pl.BlockSpec(memory_space=pltpu.VMEM),
        scratch_shapes=[
            pltpu.VMEM((2, tokens, features), BF16),
            pltpu.VMEM((2, rows, ff), BF16),
            pltpu.VMEM((2, ff, rows), BF16),
            pltpu.VMEM(block, BF16),
            pltpu.VMEM(block, BF16),
            pltpu.VMEM((2, rows, features), BF16),
            pltpu.VMEM((2, rows, features), BF16),
            pltpu.VMEM((2,) + block, BF16),
            pltpu.VMEM((3,) + block, BF16),
            pltpu.VMEM((4, 2) + block, BF16),
            pltpu.VMEM((3, 2) + block, BF16),
            pltpu.VMEM(block, BF16),
            pltpu.VMEM(block, BF16),
            pltpu.VMEM(block, F32),
            pltpu.VMEM((ff, ff), F32),
            pltpu.VMEM((ff, ff), BF16),
            pltpu.VMEM((ff, ff), BF16),
            pltpu.VMEM((1, chunk), F32),
            pltpu.SemaphoreType.DMA((4 + 2 * chunks,)),
            pltpu.SemaphoreType.DMA((2, chunks, n_experts)),
            pltpu.SemaphoreType.DMA((2, chunks, n_experts)),
            pltpu.SemaphoreType.DMA((7, 2, chunks)),
            pltpu.SemaphoreType.DMA((7, 2, chunks)),
            pltpu.SemaphoreType.REGULAR,
        ],
        compiler_params=pltpu.CompilerParams(collective_id=0, has_side_effects=True, vmem_limit_bytes=61 << 20),
        name="gossip_muon",
    )(
        out_grads[:, 0],
        routes[:, 0, :, 0],
        hiddens[:, 0, 0],
        weights[0, 0],
        tracker_offset[0, 0],
        partner_bits,
    )
    return result[None, None]


def solution(mesh):
    in_specs = (
        P(None, "site", "expert", None),
        P(None, "site", "expert", None),
        P(None, "site", "expert", None, None),
        P("site", "expert", None, None),
        P("site", "expert", None, None),
        P("site", None),
    )
    out_specs = P("site", "expert", None, None)
    return jax.shard_map(local, mesh=mesh, in_specs=in_specs, out_specs=out_specs, check_vma=False)
```
